32 devices in a mesh: group: 4 (over y, x), replica: 8 (over z, core).
Axes of the slice: x: 2, y: 2, z: 4, core: 2. Of those that a mesh axis runs over, the one named last changes fastest.
Arguments:
- inputs: bfloat16 [8, 2048, 768], P('replica', 'group'), may hold values from -6 to 6
- piece_starts: int32 [8, 4], P('replica'), may hold values from 0 to 1792, as said below
- norm1_gain: float32 [768], replicated, may hold values from 0.5 to 1.5
- norm1_bias: float32 [768], replicated, may hold values from -1.5 to 1.5
- w_query: bfloat16 [768, 768], P('group'), may hold values from -0.21875 to 0.21875
- b_query: float32 [768], replicated, may hold values from -1.5 to 1.5
- w_key: bfloat16 [768, 768], P('group'), may hold values from -0.21875 to 0.21875
- w_value: bfloat16 [768, 768], P('group'), may hold values from -0.21875 to 0.21875
- b_value: float32 [768], replicated, may hold values from -1.5 to 1.5
- subnorm1_gain: float32 [768], replicated, may hold values from 0.5 to 1.5
- subnorm1_bias: float32 [768], replicated, may hold values from -1.5 to 1.5
- w_out: bfloat16 [768, 768], P('group'), may hold values from -0.21875 to 0.21875
- b_out: float32 [768], replicated, may hold values from -1.5 to 1.5
- norm2_gain: float32 [768], replicated, may hold values from 0.5 to 1.5
- norm2_bias: float32 [768], replicated, may hold values from -1.5 to 1.5
- w_up: bfloat16 [768, 3072], P(None, 'group'), may hold values from -0.21875 to 0.21875
- b_up: float32 [3072], replicated, may hold values from -1.5 to 1.5
- subnorm2_gain: float32 [3072], replicated, may hold values from 0.5 to 1.5
- subnorm2_bias: float32 [3072], replicated, may hold values from -1.5 to 1.5
- w_down: bfloat16 [3072, 768], P('group'), may hold values from -0.109375 to 0.109375
- b_down: float32 [768], replicated, may hold values from -1.5 to 1.5
- cotangent: bfloat16 [8, 2048, 768], P('replica', 'group'), may hold values from -6 to 6
Outputs:
- outputs: bfloat16 [8, 2048, 768], P('replica', 'group')
- input_grad: bfloat16 [8, 2048, 768], P('replica', 'group')
- grad_norm1_gain: float32 [768], P(('group', 'replica'))
- grad_norm1_bias: float32 [768], P(('group', 'replica'))
- grad_w_query: float32 [768, 768], P(('group', 'replica'))
- grad_b_query: float32 [768], P(('group', 'replica'))
- grad_w_key: float32 [768, 768], P(('group', 'replica'))
- grad_w_value: float32 [768, 768], P(('group', 'replica'))
- grad_b_value: float32 [768], P(('group', 'replica'))
- grad_subnorm1_gain: float32 [768], P(('group', 'replica'))
- grad_subnorm1_bias: float32 [768], P(('group', 'replica'))
- grad_w_out: float32 [768, 768], P(('group', 'replica'))
- grad_b_out: float32 [768], P(('group', 'replica'))
- grad_norm2_gain: float32 [768], P(('group', 'replica'))
- grad_norm2_bias: float32 [768], P(('group', 'replica'))
- grad_w_up: float32 [768, 3072], P(None, ('group', 'replica'))
- grad_b_up: float32 [3072], P(('group', 'replica'))
- grad_subnorm2_gain: float32 [3072], P(('group', 'replica'))
- grad_subnorm2_bias: float32 [3072], P(('group', 'replica'))
- grad_w_down: float32 [3072, 768], P(('group', 'replica'))
- grad_b_down: float32 [768], P(('group', 'replica'))
The draws below stay inside these ranges and needn't reach their ends.
Inputs may be any that keep to these rules, and one draw needn't show every extreme that they name: `piece_starts`: in every sequence, piece i (counting from 0) starts at a position from i * 512 to (i + 1) * 512 - 256, so pieces never intersect and lie inside the sequence; in the first sequence the first piece starts at 0 and the last piece ends at the sequence's end.
All inputs are finite; a program needn't handle non-finite values.
Results may differ from the reference program's by a relative error of at most 0.015.
Values may be sent and summed in bfloat16 or wider, within the bound.
No kernel may reach another device: no remote copies, remote signals or barrier semaphores. Data moves between devices by JAX's collectives and lax.ppermute only.
A program may use at most 192 MiB of HBM per device.

```python
import jax
import jax.numpy as jnp
from jax import lax

D = 768
HEADS = 12
HEAD_DIM = 64
FF = 3072
PIECE = 256
PIECES = 4
SEQ = 2048
SEQS = 8
SEG_SHORT = 1024
SEG_MID = 2048
SEG_LONG = 2048
N_GROUP = 4


def draw_piece_starts(key, part):
    quarter = SEQ // PIECES
    anchors = jnp.arange(PIECES, dtype=jnp.int32) * quarter
    jitter = jax.random.randint(key, (SEQS, PIECES), 0, quarter - PIECE + 1, dtype=jnp.int32)
    jitter = jitter.at[0, 0].set(0)
    jitter = jitter.at[0, PIECES - 1].set(quarter - PIECE)
    return anchors[None, :] + jitter


def shard_levels(stream_key, dims, cuts, smallest, high):
    loudness = 1.0
    for position, parts in cuts:
        steps = jax.random.uniform(jax.random.fold_in(jax.random.fold_in(stream_key, 6), position), (parts,), jnp.float32, smallest / len(cuts), high / len(cuts))
        loudness = loudness * jnp.repeat(jnp.exp(steps), dims[position] // parts).reshape((-1,) + (1,) * (len(dims) - 1 - position))
    return loudness


def noise(rng, shape, scale, reach, split=(), held_as=jnp.bfloat16):
    drawn = jax.random.normal(rng, shape, jnp.float32) * scale
    if len(split) > 0:
        drawn = shard_levels(rng, shape, split, -0.22, 0.18) * drawn
    return jnp.clip(drawn, min=-reach, max=reach).astype(held_as)


def setup_inputs(seed: int = 0) -> dict:
    key_list = jax.random.split(jax.random.key(seed), 23)
    return {
        "inputs": noise(key_list[0], (SEQS, SEQ, D), 1.0, 6.0, ((0, 8), (1, 4))),
        "piece_starts": draw_piece_starts(jax.random.fold_in(key_list[22], 71), 0),
        "norm1_gain": jnp.clip(1.0 + 0.1 * jax.random.normal(key_list[2], (D,), jnp.float32), 0.5, 1.5),
        "norm1_bias": noise(key_list[3], (D,), 0.3, 1.5, (), jnp.float32),
        "w_query": noise(key_list[4], (D, D), D ** -0.5, 0.21875, ((0, 4),)),
        "b_query": noise(key_list[5], (D,), 0.3, 1.5, (), jnp.float32),
        "w_key": noise(key_list[6], (D, D), D ** -0.5, 0.21875, ((0, 4),)),
        "w_value": noise(key_list[7], (D, D), D ** -0.5, 0.21875, ((0, 4),)),
        "b_value": noise(key_list[8], (D,), 0.3, 1.5, (), jnp.float32),
        "subnorm1_gain": jnp.clip(1.0 + 0.1 * jax.random.normal(key_list[9], (D,), jnp.float32), 0.5, 1.5),
        "subnorm1_bias": noise(key_list[10], (D,), 0.3, 1.5, (), jnp.float32),
        "w_out": noise(key_list[11], (D, D), D ** -0.5, 0.21875, ((0, 4),)),
        "b_out": noise(key_list[12], (D,), 0.3, 1.5, (), jnp.float32),
        "norm2_gain": jnp.clip(1.0 + 0.1 * jax.random.normal(key_list[13], (D,), jnp.float32), 0.5, 1.5),
        "norm2_bias": noise(key_list[14], (D,), 0.3, 1.5, (), jnp.float32),
        "w_up": noise(key_list[15], (D, FF), D ** -0.5, 0.21875, ((1, 4),)),
        "b_up": noise(key_list[16], (FF,), 0.3, 1.5, (), jnp.float32),
        "subnorm2_gain": jnp.clip(1.0 + 0.1 * jax.random.normal(key_list[17], (FF,), jnp.float32), 0.5, 1.5),
        "subnorm2_bias": noise(key_list[18], (FF,), 0.3, 1.5, (), jnp.float32),
        "w_down": noise(key_list[19], (FF, D), FF ** -0.5, 0.109375, ((0, 4),)),
        "b_down": noise(key_list[20], (D,), 0.3, 1.5, (), jnp.float32),
        "cotangent": noise(key_list[21], (SEQS, SEQ, D), 1.0, 6.0, ((0, 8), (1, 4))),
    }


@jax.custom_vjp
def low(v):
    return lax.optimization_barrier(v.astype(jnp.bfloat16)).astype(jnp.float32)

@jax.custom_vjp
def low_back(v):
    return v

def low_keep(v):
    return (low(v), None)

def low_pass(kept, grad):
    return (grad,)

def back_keep(v):
    return (v, None)

def back_low(kept, grad):
    return (low(grad),)
low.defvjp(low_keep, low_pass)
low_back.defvjp(back_keep, back_low)
DILATIONS = (1, 2, 4, 8, 16)
EPSILON = 1e-05

def matmul(left_matrix, right_matrix):
    return jnp.dot(left_matrix, right_matrix, preferred_element_type=jnp.float32, precision=lax.Precision.HIGHEST)

def layer_norm(values, gains, biases):
    average = lax.optimization_barrier(jnp.mean(values, axis=-1, keepdims=True))
    centered = values - average
    variance = lax.optimization_barrier(jnp.mean(centered * centered, axis=-1, keepdims=True))
    return centered * lax.rsqrt(variance + EPSILON) * gains + biases

def piece_index(positions, starts):
    inside = (positions[:, None] >= starts[None, :]) & (positions[:, None] < starts[None, :] + PIECE)
    numbers = jnp.arange(starts.shape[0], dtype=jnp.int32)
    return lax.optimization_barrier(jnp.max(jnp.where(inside, numbers[None, :], -1), axis=1)).astype(jnp.int32)

def multiplicity(query_pos, key_pos, query_piece, key_piece, head_index, segments):
    allowed = (key_pos[None, :] <= query_pos[:, None]) | (query_piece[:, None] == key_piece[None, :]) & (query_piece[:, None] >= 0)
    counted = jnp.zeros(allowed.shape, jnp.float32)
    for segment, dilation in zip(segments, DILATIONS):
        offset = head_index % dilation
        together = query_pos[:, None] // segment == key_pos[None, :] // segment
        picked = (query_pos % dilation == offset)[:, None] & (key_pos % dilation == offset)[None, :]
        counted = counted + (together & picked & allowed).astype(jnp.float32)
    return counted

def block_attend(block_q, row_start, key_head, value_head, head_index, pieces, segments):
    row_count = block_q.shape[0]
    seq_len = key_head.shape[0]
    query_pos = row_start + jnp.arange(row_count, dtype=jnp.int32)
    key_pos = jnp.arange(seq_len, dtype=jnp.int32)
    query_piece = lax.dynamic_slice_in_dim(pieces, row_start, row_count)
    counted = multiplicity(query_pos, key_pos, query_piece, pieces, head_index, segments)
    scores = low_back(matmul(block_q, key_head.T) * HEAD_DIM ** (-0.5))
    live_mask = counted > 0
    row_max = lax.optimization_barrier(jnp.max(jnp.where(live_mask, scores, -1e+30), axis=1, keepdims=True))
    powered = counted * jnp.exp(jnp.where(live_mask, scores, row_max) - row_max)
    probabilities = low(powered / lax.optimization_barrier(jnp.sum(powered, axis=1, keepdims=True)))
    return matmul(probabilities, value_head)

def attention(queries_part, row_offset, keys, values, pieces):
    part_len = queries_part.shape[0]
    seq_len = keys.shape[0]
    segments = (SEG_SHORT, SEG_MID, SEG_LONG, SEG_LONG, SEG_LONG)
    block_rows = min(512, part_len)
    count_blocks = part_len // block_rows

    def split_heads(matrix):
        return matrix.reshape(matrix.shape[0], HEADS, HEAD_DIM).transpose(1, 0, 2)

    def one_head(packed):
        head_q, head_k, head_v, head_index = packed

        def one_block(inner_item):
            block_q, row_start = inner_item
            return block_attend(block_q, row_start, head_k, head_v, head_index, pieces, segments)
        blocks_q = head_q.reshape(count_blocks, block_rows, HEAD_DIM)
        block_starts = row_offset + jnp.arange(count_blocks, dtype=jnp.int32) * block_rows
        return lax.map(jax.checkpoint(one_block), (blocks_q, block_starts)).reshape(part_len, HEAD_DIM)
    head_numbers = jnp.arange(HEADS, dtype=jnp.int32)
    per_head = lax.map(jax.checkpoint(one_head), (split_heads(queries_part), split_heads(keys), split_heads(values), head_numbers))
    return per_head.transpose(1, 0, 2).reshape(part_len, HEADS * HEAD_DIM)

def forward_sequence(sequence, starts, params):
    norm1_gain, norm1_bias, w_query, b_query, w_key, w_value, b_value, subnorm1_gain, subnorm1_bias, w_out, b_out, norm2_gain, norm2_bias, w_up, b_up, subnorm2_gain, subnorm2_bias, w_down, b_down = params
    seq_len = sequence.shape[0]
    positions = jnp.arange(seq_len, dtype=jnp.int32)
    pieces = piece_index(positions, starts)
    normed = low(layer_norm(sequence, norm1_gain, norm1_bias))
    queries = low(low_back(matmul(normed, w_query) + b_query))
    keys = low(low_back(matmul(normed, w_key)))
    values = low(low_back(matmul(normed, w_value) + b_value))
    part_len = seq_len // N_GROUP
    parts_out = []
    for group_number in range(N_GROUP):
        keys_copy = low_back(keys)
        values_copy = low_back(values)
        queries_part = queries[group_number * part_len:(group_number + 1) * part_len]
        parts_out.append(attention(queries_part, group_number * part_len, keys_copy, values_copy, pieces))
    attended = low_back(jnp.concatenate(parts_out, axis=0))
    mixed_in = low(layer_norm(attended, subnorm1_gain, subnorm1_bias))
    branch = low_back(matmul(mixed_in, w_out) + b_out)
    middle = sequence + branch
    normed_mid = low(layer_norm(middle, norm2_gain, norm2_bias))
    hidden_pre = low_back(matmul(normed_mid, w_up) + b_up)
    hidden_act = jax.nn.gelu(hidden_pre, approximate=False)
    hidden_in = low(layer_norm(hidden_act, subnorm2_gain, subnorm2_bias))
    ffn_out = low_back(matmul(hidden_in, w_down) + b_down)
    return middle + ffn_out

def reference(inputs, piece_starts, norm1_gain, norm1_bias, w_query, b_query, w_key, w_value, b_value, subnorm1_gain, subnorm1_bias, w_out, b_out, norm2_gain, norm2_bias, w_up, b_up, subnorm2_gain, subnorm2_bias, w_down, b_down, cotangent):
    params = tuple((parameter.astype(jnp.float32) for parameter in (norm1_gain, norm1_bias, w_query, b_query, w_key, w_value, b_value, subnorm1_gain, subnorm1_bias, w_out, b_out, norm2_gain, norm2_bias, w_up, b_up, subnorm2_gain, subnorm2_bias, w_down, b_down)))

    def one_sequence(grad_totals, element):
        sequence, starts, seq_cotangent = element

        def run_forward(seq_values, param_values):
            return forward_sequence(seq_values, starts, param_values)
        result, pullback = jax.vjp(run_forward, sequence.astype(jnp.float32), params)
        grad_sequence, grad_params = pullback(seq_cotangent.astype(jnp.float32))
        new_totals = jax.tree.map(lambda total_part, new_part: total_part + new_part, grad_totals, grad_params)
        return (new_totals, (result.astype(jnp.bfloat16), grad_sequence.astype(jnp.bfloat16)))
    zero_grads = jax.tree.map(jnp.zeros_like, params)
    totals, (outputs, input_grad) = lax.scan(one_sequence, zero_grads, (inputs, piece_starts, cotangent))
    grad_norm1_gain, grad_norm1_bias, grad_w_query, grad_b_query, grad_w_key, grad_w_value, grad_b_value, grad_subnorm1_gain, grad_subnorm1_bias, grad_w_out, grad_b_out, grad_norm2_gain, grad_norm2_bias, grad_w_up, grad_b_up, grad_subnorm2_gain, grad_subnorm2_bias, grad_w_down, grad_b_down = totals
    return (outputs, input_grad, grad_norm1_gain, grad_norm1_bias, grad_w_query, grad_b_query, grad_w_key, grad_w_value, grad_b_value, grad_subnorm1_gain, grad_subnorm1_bias, grad_w_out, grad_b_out, grad_norm2_gain, grad_norm2_bias, grad_w_up, grad_b_up, grad_subnorm2_gain, grad_subnorm2_bias, grad_w_down, grad_b_down)
```

```python
import functools

import jax
import jax.numpy as jnp
from jax import lax
from jax.experimental import pallas as pl
from jax.experimental.pallas import tpu as pltpu
from jax.sharding import PartitionSpec as P

HEAD_DIM = 64
PIECE = 256
HALF = 256
EPSILON = 1e-05
F32 = jnp.float32
BF16 = jnp.bfloat16
NEG = -1e30


def dot_nt(left, right):
    return lax.dot_general(left, right, (((1,), (1,)), ((), ())), preferred_element_type=F32)


def dot_nn(left, right):
    return lax.dot_general(left, right, (((1,), (0,)), ((), ())), preferred_element_type=F32)


def dot_tn(left, right):
    return lax.dot_general(left, right, (((0,), (0,)), ((), ())), preferred_element_type=F32)


def level_weights(parity, head, axis):
    shape = (HALF, 1) if axis == 0 else (1, HALF)
    pos = 2 * lax.broadcasted_iota(jnp.int32, shape, axis) + parity
    diff = pos - head + 16
    count = jnp.zeros(shape, F32)
    for dilation in (2, 4, 8, 16):
        count = count + jnp.where((diff & (dilation - 1)) == 0, 1.0, 0.0).astype(F32)
    return count


def build_mask(start, parity_k, parity_q):
    key = 2 * lax.broadcasted_iota(jnp.int32, (HALF, HALF), 0) + parity_k
    query = 2 * lax.broadcasted_iota(jnp.int32, (HALF, HALF), 1) + parity_q
    in_key = (key >= start) & (key < start + PIECE)
    in_query = (query >= start) & (query < start + PIECE)
    allowed = (key <= query) | (in_key & in_query)
    return jnp.where(allowed, 0.0, NEG).astype(F32)


def fill_masks(starts_ref, mask_s, mask_o):
    def step(index, carry):
        block = index // 2
        parity = index % 2
        start = starts_ref[block] - block * 2 * HALF
        mask_s[index] = build_mask(start, parity, parity)
        mask_o[index] = build_mask(start, 1 - parity, parity)
        return carry

    lax.fori_loop(0, 8, step, 0)


def fill_logs(head, log_w, log_x):
    match = head % 2
    for parity in range(2):
        low = jnp.minimum(level_weights(parity, head, 0), level_weights(parity, head, 1))
        log_w[parity] = jnp.log(1.0 + low)
    low = jnp.minimum(level_weights(match, head, 0), level_weights(match, head, 1))
    log_x[...] = jnp.log(jnp.maximum(low, 1.0))


def attention_forward_kernel(
    info_ref, starts_ref, a0, a1, a2, a3, o0, o1, o2, o3, f0, f1, f2, f3, lse_ref,
    qs, ks, vt, os, mask_s, mask_o, log_w, log_x, m_c, l_c, acc_c,
):
    step_head = pl.program_id(0)
    group = info_ref[0]
    head = 3 * group + step_head
    match = head % 2
    parts = (a0, a1, a2, a3)

    @pl.when(step_head == 0)
    def _():
        fill_masks(starts_ref, mask_s, mask_o)

    fill_logs(head, log_w, log_x)
    for j in range(3):

        @pl.when(step_head == j)
        def _():
            for k in range(4):
                block = lax.bitwise_xor(group, k)
                for p in range(2):
                    rows = slice(p * HALF, (p + 1) * HALF)
                    qs[2 * block + p] = parts[k][rows, j * 64 : j * 64 + 64]
                    ks[2 * block + p] = parts[k][rows, 192 + j * 64 : 256 + j * 64]
                    vt[2 * block + p] = parts[k][rows, 384 + j * 64 : 448 + j * 64].T

    def finish(slot, m_prev, l_prev, acc_prev, scores, values):
        top = m_prev
        for part in scores:
            top = jnp.maximum(top, jnp.max(part, axis=0, keepdims=True))
        scale = jnp.exp(m_prev - top)
        total = l_prev * scale
        acc = acc_prev * scale
        for part, value in zip(scores, values):
            power = jnp.exp(part - top)
            total = total + jnp.sum(power, axis=0, keepdims=True)
            acc = acc + dot_nn(value, power.astype(BF16))
        return top, total, acc

    def body(index, carry):
        half_seq = index // 2
        parity = index % 2
        first = 4 * half_seq
        slot_a = first + parity
        slot_b = first + 2 + parity
        m_c[...] = jnp.full(m_c.shape, NEG, F32)
        l_c[...] = jnp.zeros(l_c.shape, F32)
        acc_c[...] = jnp.zeros(acc_c.shape, F32)

        @pl.when((half_seq == 1) & (parity == match))
        def _():
            for n, slot in ((0, slot_a), (1, slot_b)):
                query = qs[slot]
                scores = [dot_nt(ks[2 * b + match], query) + log_x[...] for b in range(2)]
                top, total, acc = finish(
                    slot,
                    jnp.full((1, HALF), NEG, F32),
                    jnp.zeros((1, HALF), F32),
                    jnp.zeros((HEAD_DIM, HALF), F32),
                    scores,
                    [vt[match], vt[2 + match]],
                )
                m_c[n] = top
                l_c[n] = total
                acc_c[n] = acc

        same_a, other_a = slot_a, first + 1 - parity
        same_b, other_b = slot_b, first + 3 - parity
        logs = log_w[parity]
        query = qs[slot_a]
        scores = [
            dot_nt(ks[same_a], query) + (mask_s[slot_a] + logs),
            dot_nt(ks[other_a], query) + mask_o[slot_a],
        ]
        top, total, acc = finish(
            slot_a, m_c[0], l_c[0], acc_c[0], scores, [vt[same_a], vt[other_a]]
        )
        os[slot_a] = (acc / total).T
        lse_ref[0, pl.ds(slot_a, 1), :] = top + jnp.log(total)
        query = qs[slot_b]
        scores = [
            dot_nt(ks[same_a], query) + logs,
            dot_nt(ks[other_a], query),
            dot_nt(ks[same_b], query) + (mask_s[slot_b] + logs),
            dot_nt(ks[other_b], query) + mask_o[slot_b],
        ]
        top, total, acc = finish(
            slot_b, m_c[1], l_c[1], acc_c[1], scores,
            [vt[same_a], vt[other_a], vt[same_b], vt[other_b]],
        )
        os[slot_b] = (acc / total).T
        lse_ref[0, pl.ds(slot_b, 1), :] = top + jnp.log(total)
        return carry

    lax.fori_loop(0, 4, body, 0)
    for j in range(3):

        @pl.when(step_head == j)
        def _():
            for k, (low, full) in enumerate(((o0, f0), (o1, f1), (o2, f2), (o3, f3))):
                block = lax.bitwise_xor(group, k)
                for p in range(2):
                    rows = slice(p * HALF, (p + 1) * HALF)
                    result = os[2 * block + p]
                    full[rows, j * 64 : j * 64 + 64] = result
                    low[rows, j * 64 : j * 64 + 64] = result.astype(BF16)


def attention_backward_kernel(
    info_ref, starts_ref, a0, a1, a2, a3, d0, d1, d2, d3, f0, f1, f2, f3, lse_ref, g0, g1, g2, g3,
    qs, ks, vs, kt, ds, delta, gq, gk, gv, mask_s, mask_o, log_w, log_x,
):
    step_head = pl.program_id(0)
    group = info_ref[0]
    head = 3 * group + step_head
    match = head % 2

    @pl.when(step_head == 0)
    def _():
        fill_masks(starts_ref, mask_s, mask_o)

    fill_logs(head, log_w, log_x)
    for j in range(3):

        @pl.when(step_head == j)
        def _():
            for k, (part, grad, full) in enumerate(
                ((a0, d0, f0), (a1, d1, f1), (a2, d2, f2), (a3, d3, f3))
            ):
                block = lax.bitwise_xor(group, k)
                for p in range(2):
                    rows = slice(p * HALF, (p + 1) * HALF)
                    slot = 2 * block + p
                    qs[slot] = part[rows, j * 64 : j * 64 + 64]
                    key = part[rows, 192 + j * 64 : 256 + j * 64]
                    ks[slot] = key
                    kt[slot] = key.T
                    vs[slot] = part[rows, 384 + j * 64 : 448 + j * 64]
                    up = grad[rows, j * 64 : j * 64 + 64]
                    ds[slot] = up
                    product = up.astype(F32) * full[rows, j * 64 : j * 64 + 64]
                    delta[slot] = jnp.sum(product.T, axis=0, keepdims=True)

    gk[...] = jnp.zeros(gk.shape, F32)
    gv[...] = jnp.zeros(gv.shape, F32)

    def tile(slot_k, query, grad, lse, dlt, bias):
        scores = dot_nt(ks[slot_k], query)
        if bias is not None:
            scores = scores + bias
        prob = jnp.exp(scores - lse)
        grad_prob = dot_nt(vs[slot_k], grad)
        grad_score = (prob * (grad_prob - dlt)).astype(BF16)
        gv[slot_k] += dot_nn(prob.astype(BF16), grad)
        gk[slot_k] += dot_nn(grad_score, query)
        return dot_nn(kt[slot_k], grad_score)

    def body(index, carry):
        half_seq = index // 2
        parity = index % 2
        first = 4 * half_seq
        slot_a = first + parity
        slot_b = first + 2 + parity
        same_a, other_a = slot_a, first + 1 - parity
        same_b, other_b = slot_b, first + 3 - parity
        logs = log_w[parity]
        args = (qs[slot_a], ds[slot_a], lse_ref[0, pl.ds(slot_a, 1), :], delta[slot_a])
        total = tile(same_a, *args, mask_s[slot_a] + logs)
        total = total + tile(other_a, *args, mask_o[slot_a])
        gq[slot_a] = total
        args = (qs[slot_b], ds[slot_b], lse_ref[0, pl.ds(slot_b, 1), :], delta[slot_b])
        total = tile(same_a, *args, logs)
        total = total + tile(other_a, *args, None)
        total = total + tile(same_b, *args, mask_s[slot_b] + logs)
        total = total + tile(other_b, *args, mask_o[slot_b])
        gq[slot_b] = total

        @pl.when((half_seq == 1) & (parity == match))
        def _():
            for slot in (slot_a, slot_b):
                args = (qs[slot], ds[slot], lse_ref[0, pl.ds(slot, 1), :], delta[slot])
                more = tile(match, *args, log_x[...])
                more = more + tile(2 + match, *args, log_x[...])
                gq[slot] += more

        return carry

    lax.fori_loop(0, 4, body, 0)
    for j in range(3):

        @pl.when(step_head == j)
        def _():
            for k, out in enumerate((g0, g1, g2, g3)):
                block = lax.bitwise_xor(group, k)
                for p in range(2):
                    rows = slice(p * HALF, (p + 1) * HALF)
                    slot = 2 * block + p
                    scaled = gq[slot] * (HEAD_DIM ** (-0.5))
                    out[rows, j * 64 : j * 64 + 64] = scaled.T.astype(BF16)
                    out[rows, 192 + j * 64 : 256 + j * 64] = gk[slot].astype(BF16)
                    out[rows, 384 + j * 64 : 448 + j * 64] = gv[slot].astype(BF16)


def whole(shape):
    return pl.BlockSpec(shape, lambda j: (0,) * len(shape))


def smem():
    return pl.BlockSpec(memory_space=pltpu.SMEM)


def attention_forward(info, starts, parts):
    rows = parts[0].shape[0]
    head_spec = pl.BlockSpec((1, 8, HALF), lambda j: (j, 0, 0))
    out = pl.pallas_call(
        attention_forward_kernel,
        grid=(3,),
        in_specs=[smem(), smem()] + [whole((rows, 576))] * 4,
        out_specs=[whole((rows, 192))] * 8 + [head_spec],
        out_shape=[jax.ShapeDtypeStruct((rows, 192), BF16)] * 4
        + [jax.ShapeDtypeStruct((rows, 192), F32)] * 4
        + [jax.ShapeDtypeStruct((3, 8, HALF), F32)],
        scratch_shapes=[
            pltpu.VMEM((8, HALF, HEAD_DIM), BF16),
            pltpu.VMEM((8, HALF, HEAD_DIM), BF16),
            pltpu.VMEM((8, HEAD_DIM, HALF), BF16),
            pltpu.VMEM((8, HALF, HEAD_DIM), F32),
            pltpu.VMEM((8, HALF, HALF), F32),
            pltpu.VMEM((8, HALF, HALF), F32),
            pltpu.VMEM((2, HALF, HALF), F32),
            pltpu.VMEM((HALF, HALF), F32),
            pltpu.VMEM((2, 1, HALF), F32),
            pltpu.VMEM((2, 1, HALF), F32),
            pltpu.VMEM((2, HEAD_DIM, HALF), F32),
        ],
        name="attention_forward",
    )(info, starts, *parts)
    return out[0:4], out[4:8], out[8]


def attention_backward(info, starts, parts, grads, full, lse):
    rows = parts[0].shape[0]
    head_spec = pl.BlockSpec((1, 8, HALF), lambda j: (j, 0, 0))
    return pl.pallas_call(
        attention_backward_kernel,
        grid=(3,),
        in_specs=[smem(), smem()]
        + [whole((rows, 576))] * 4
        + [whole((rows, 192))] * 8
        + [head_spec],
        out_specs=[whole((rows, 576))] * 4,
        out_shape=[jax.ShapeDtypeStruct((rows, 576), BF16)] * 4,
        scratch_shapes=[
            pltpu.VMEM((8, HALF, HEAD_DIM), BF16),
            pltpu.VMEM((8, HALF, HEAD_DIM), BF16),
            pltpu.VMEM((8, HALF, HEAD_DIM), BF16),
            pltpu.VMEM((8, HEAD_DIM, HALF), BF16),
            pltpu.VMEM((8, HALF, HEAD_DIM), BF16),
            pltpu.VMEM((8, 1, HALF), F32),
            pltpu.VMEM((8, HEAD_DIM, HALF), F32),
            pltpu.VMEM((8, HALF, HEAD_DIM), F32),
            pltpu.VMEM((8, HALF, HEAD_DIM), F32),
            pltpu.VMEM((8, HALF, HALF), F32),
            pltpu.VMEM((8, HALF, HALF), F32),
            pltpu.VMEM((2, HALF, HALF), F32),
            pltpu.VMEM((HALF, HALF), F32),
        ],
        name="attention_backward",
    )(info, starts, *parts, *grads, *full, lse)


def xor_pairs(axis, step):
    return [(i, i ^ step) for i in range(lax.axis_size(axis))]


def swap(array, axis, step):
    return lax.ppermute(array, axis, xor_pairs(axis, step))


def pick(array, index, axis=0):
    return lax.dynamic_index_in_dim(array, index, axis, keepdims=False)


def gather_relative(shard, core):
    rows = shard.shape[0] // 2
    mine = pick(shard.reshape((2, rows) + shard.shape[1:]), core)
    result = [shard]
    for k in (1, 2, 3):
        got = swap(mine, "group", k)
        other = swap(got, "replica", 1)
        result.append(
            jnp.where(core == 0, jnp.concatenate([got, other]), jnp.concatenate([other, got]))
        )
    return result


def to_absolute(parts, group):
    out = jnp.zeros((4,) + parts[0].shape, parts[0].dtype)
    for k, part in enumerate(parts):
        out = lax.dynamic_update_index_in_dim(out, part, group ^ k, 0)
    return out


def relative_columns(vector, group):
    chunks = vector.reshape(4, -1)
    return jnp.concatenate([pick(chunks, group ^ k) for k in range(4)])


def absolute_columns(vector, group):
    return relative_columns(vector, group)


def evens_first(array):
    rows = array.shape[0]
    return array.reshape(rows // 2, 2, -1).transpose(1, 0, 2).reshape(rows, -1)


def natural_order(array):
    rows = array.shape[0]
    return array.reshape(2, rows // 2, -1).transpose(1, 0, 2).reshape(rows, -1)


def reduce_replica(array, replica, scatter_axis, bits):
    for n in range(bits):
        axis = scatter_axis + bits - 1 - n
        bit = (replica >> (n + 1)) & 1
        send = pick(array, 1 - bit, axis).astype(BF16)
        keep = pick(array, bit, axis)
        got = swap(send, "replica", 2 << n)
        array = keep.astype(F32) + got.astype(F32)
    return array


def norm_parts(values):
    average = jnp.mean(values, axis=-1, keepdims=True)
    centered = values - average
    variance = jnp.mean(centered * centered, axis=-1, keepdims=True)
    rate = lax.rsqrt(variance + EPSILON)
    return centered * rate, rate


def layer_norm(values, gains, biases):
    normal, rate = norm_parts(values)
    return normal * gains + biases


def norm_backward(values, gains, upstream):
    normal, rate = norm_parts(values)
    scaled = upstream * gains
    mean_scaled = jnp.mean(scaled, axis=-1, keepdims=True)
    mean_product = jnp.mean(scaled * normal, axis=-1, keepdims=True)
    grad = rate * (scaled - mean_scaled - normal * mean_product)
    return grad, jnp.sum(upstream * normal, axis=0), jnp.sum(upstream, axis=0)


def gelu_exact(values):
    return jax.nn.gelu(values, approximate=False)


def body(
    inputs,
    piece_starts,
    norm1_gain,
    norm1_bias,
    w_query,
    b_query,
    w_key,
    w_value,
    b_value,
    subnorm1_gain,
    subnorm1_bias,
    w_out,
    b_out,
    norm2_gain,
    norm2_bias,
    w_up,
    b_up,
    subnorm2_gain,
    subnorm2_bias,
    w_down,
    b_down,
    cotangent,
):
    rows = inputs.shape[1]
    model_dim = inputs.shape[2]
    hidden_dim = b_up.shape[0]
    replicas = lax.axis_size("replica")
    bits = (replicas // 2).bit_length() - 1
    group = lax.axis_index("group")
    replica = lax.axis_index("replica")
    core = replica % 2
    half = model_dim // 2
    width = model_dim // 4
    info = group.reshape(1).astype(jnp.int32)
    starts = piece_starts[0]

    source_low = evens_first(inputs[0])
    source = source_low.astype(F32)
    normed = layer_norm(source, norm1_gain, norm1_bias).astype(BF16)
    shard = jnp.concatenate(
        [w.reshape(width, 4, width).transpose(1, 0, 2) for w in (w_query, w_key, w_value)], axis=2
    )
    columns = [pick(shard, group)]
    columns += [swap(pick(shard, group ^ k), "group", k) for k in (1, 2, 3)]
    blocks = [normed] + [swap(normed, "group", k) for k in (1, 2, 3)]
    w_own = to_absolute(columns, group).reshape(model_dim, 3 * width)
    b_own = jnp.concatenate(
        [
            pick(b_query.reshape(4, width), group),
            jnp.zeros((width,), F32),
            pick(b_value.reshape(4, width), group),
        ]
    )
    scale_own = jnp.concatenate(
        [jnp.full((width,), HEAD_DIM ** (-0.5), F32), jnp.ones((2 * width,), F32)]
    )
    parts = [((dot_nn(block, w_own) + b_own) * scale_own).astype(BF16) for block in blocks]

    out_rel = gather_relative(w_out, core)
    up_rel = gather_relative(w_up.T, core)
    down_rel = gather_relative(w_down, core)
    qkv_rel = gather_relative(shard.transpose(1, 0, 2), core)

    heads_low, heads_full, lse = attention_forward(info, starts, parts)
    attended_rel = [heads_low[0]] + [swap(heads_low[k], "group", k) for k in (1, 2, 3)]
    attended = jnp.concatenate(attended_rel, axis=1).astype(F32)
    gain_s1 = relative_columns(subnorm1_gain, group)
    bias_s1 = relative_columns(subnorm1_bias, group)
    mixed_in = layer_norm(attended, gain_s1, bias_s1).astype(BF16)
    out_full = jnp.concatenate(out_rel, axis=0)
    middle = source + dot_nn(mixed_in, out_full) + b_out
    normed_mid = layer_norm(middle, norm2_gain, norm2_bias).astype(BF16)
    up_full = jnp.concatenate(up_rel, axis=0)
    down_full = jnp.concatenate(down_rel, axis=0)
    b_up_rel = relative_columns(b_up, group)
    gain_s2 = relative_columns(subnorm2_gain, group)
    bias_s2 = relative_columns(subnorm2_bias, group)
    hidden_pre = dot_nt(normed_mid, up_full) + b_up_rel
    hidden_act = gelu_exact(hidden_pre)
    hidden_in = layer_norm(hidden_act, gain_s2, bias_s2).astype(BF16)
    outputs = (middle + dot_nn(hidden_in, down_full) + b_down).astype(BF16)

    upstream_low = evens_first(cotangent[0])
    upstream = upstream_low.astype(F32)
    grad_b_down = jnp.sum(upstream, axis=0)

    def halves(matrix):
        chunks = matrix.reshape(rows, 2, half).transpose(1, 0, 2)
        return pick(chunks, core), pick(chunks, 1 - core)

    def start_reduce(left, right):
        keep, send = halves(right)
        got = swap(dot_tn(left, send).astype(BF16), "replica", 1)
        return dot_tn(left, keep) + got.astype(F32)

    def group_reduce(grad, order):
        grad = grad.reshape(2, 2, -1, half)
        for step in order:
            if step == 1:
                axis = grad.ndim - 3
            else:
                axis = 0
            send = lax.index_in_dim(grad, 1, axis, keepdims=False).astype(BF16)
            keep = lax.index_in_dim(grad, 0, axis, keepdims=False)
            grad = keep.astype(F32) + swap(send, "group", step).astype(F32)
        return grad

    def finish_reduce(grads):
        pieces = [grad.reshape((2,) * (bits + 1) + (-1, half)) for grad in grads]
        counts = [piece.shape[-2] for piece in pieces]
        joined = reduce_replica(jnp.concatenate(pieces, axis=-2), replica, 0, bits)
        send = pick(joined, 1 - core).astype(BF16)
        keep = pick(joined, core)
        got = swap(send, "replica", 1).astype(F32)
        full = jnp.where(
            core == 0,
            jnp.concatenate([keep, got], axis=1),
            jnp.concatenate([got, keep], axis=1),
        )
        out = []
        offset = 0
        for count in counts:
            out.append(lax.slice_in_dim(full, offset, offset + count, axis=0))
            offset += count
        return out

    red_down = group_reduce(start_reduce(hidden_in, upstream_low), (1, 2))
    grad_act, grad_subnorm2_gain, grad_subnorm2_bias = norm_backward(
        hidden_act, gain_s2, dot_nt(upstream_low, down_full)
    )
    act_value, act_pull = jax.vjp(gelu_exact, hidden_pre)
    grad_pre = act_pull(grad_act)[0].astype(BF16)
    red_up = group_reduce(start_reduce(grad_pre, normed_mid), (2, 1))
    grad_b_up = jnp.sum(grad_pre.astype(F32), axis=0)
    grad_mid_norm, grad_norm2_gain, grad_norm2_bias = norm_backward(
        middle, norm2_gain, dot_nn(grad_pre, up_full)
    )
    grad_middle = upstream + grad_mid_norm
    grad_branch = grad_middle.astype(BF16)
    red_out = group_reduce(start_reduce(mixed_in, grad_branch), (1, 2))
    grad_b_out = jnp.sum(grad_branch.astype(F32), axis=0)
    grad_attended_full, grad_subnorm1_gain, grad_subnorm1_bias = norm_backward(
        attended, gain_s1, dot_nt(grad_branch, out_full)
    )
    grad_attended = grad_attended_full.astype(BF16)

    grad_rel = [grad_attended[:, k * width : (k + 1) * width] for k in range(4)]
    grad_heads = [grad_rel[0]] + [swap(grad_rel[k], "group", k) for k in (1, 2, 3)]
    grads = attention_backward(info, starts, parts, grad_heads, heads_full, lse)
    tokens = [grads[0]] + [swap(grads[k], "group", k) for k in (1, 2, 3)]

    grad_w = dot_tn(blocks[0], grads[0])
    column_sums = jnp.sum(grads[0].astype(F32), axis=0)
    for k in (1, 2, 3):
        grad_w = grad_w + dot_tn(blocks[k], grads[k])
        column_sums = column_sums + jnp.sum(grads[k].astype(F32), axis=0)
    grad_w = grad_w.reshape((4,) + (2,) * bits + (2, -1, 3 * width))
    core_axis = 1 + bits
    got = swap(pick(grad_w, 1 - core, core_axis).astype(BF16), "replica", 1)
    grad_w = pick(grad_w, core, core_axis) + got.astype(F32)
    grad_w = reduce_replica(grad_w, replica, 1, bits)
    pieces = [pick(grad_w, group)]
    pieces += [swap(pick(grad_w, group ^ k).astype(BF16), "group", k).astype(F32) for k in (1, 2, 3)]
    qkv_grads = to_absolute(pieces, group)
    qkv_grads = qkv_grads.reshape(4, -1, 3, width).transpose(2, 1, 0, 3).reshape(3, -1, model_dim)

    rows_abs = to_absolute(qkv_rel, group).reshape(model_dim, 4, 3 * width)
    grad_normed = jnp.zeros((rows, model_dim), F32)
    for k in range(4):
        grad_normed = grad_normed + dot_nt(tokens[k], pick(rows_abs, group ^ k, 1))
    grad_source, grad_norm1_gain, grad_norm1_bias = norm_backward(source, norm1_gain, grad_normed)
    input_grad = natural_order((grad_middle + grad_source).astype(BF16))[None]
    outputs = natural_order(outputs)[None]

    grad_w_down, grad_w_up, grad_w_out = finish_reduce([red_down, red_up, red_out])

    own_block = lax.broadcasted_iota(jnp.int32, (4, 1), 0) == group

    def spread(sums):
        return jnp.where(own_block, sums[None, :], 0.0).reshape(-1)

    vectors = [
        grad_norm1_gain,
        grad_norm1_bias,
        spread(column_sums[:width]),
        spread(column_sums[2 * width :]),
        absolute_columns(grad_subnorm1_gain, group),
        absolute_columns(grad_subnorm1_bias, group),
        grad_b_out,
        grad_norm2_gain,
        grad_norm2_bias,
        absolute_columns(grad_b_up, group),
        absolute_columns(grad_subnorm2_gain, group),
        absolute_columns(grad_subnorm2_bias, group),
        grad_b_down,
    ]
    owners = 4 * replicas
    sizes = [vector.shape[0] // owners for vector in vectors]
    packed = jnp.concatenate([vector.reshape(owners, -1) for vector in vectors], axis=1)
    packed = lax.all_to_all(packed, ("group", "replica"), 0, 0, tiled=True)
    summed = jnp.sum(packed, axis=0)
    out = []
    offset = 0
    for size in sizes:
        out.append(lax.slice_in_dim(summed, offset, offset + size))
        offset += size
    (
        grad_norm1_gain, grad_norm1_bias, grad_b_query, grad_b_value, grad_subnorm1_gain,
        grad_subnorm1_bias, grad_b_out, grad_norm2_gain, grad_norm2_bias, grad_b_up,
        grad_subnorm2_gain, grad_subnorm2_bias, grad_b_down,
    ) = out
    return (
        outputs,
        input_grad,
        grad_norm1_gain,
        grad_norm1_bias,
        qkv_grads[0],
        grad_b_query,
        qkv_grads[1],
        qkv_grads[2],
        grad_b_value,
        grad_subnorm1_gain,
        grad_subnorm1_bias,
        grad_w_out,
        grad_b_out,
        grad_norm2_gain,
        grad_norm2_bias,
        grad_w_up.T,
        grad_b_up,
        grad_subnorm2_gain,
        grad_subnorm2_bias,
        grad_w_down,
        grad_b_down,
    )


def solution(mesh):
    tokens = P("replica", "group", None)
    rows = P("group", None)
    none = P()
    both = ("group", "replica")
    in_specs = (
        tokens, P("replica", None), none, none, rows, none, rows, rows, none, none, none, rows,
        none, none, none, P(None, "group"), none, none, none, rows, none, tokens,
    )
    vec = P(both)
    mat = P(both, None)
    out_specs = (
        tokens, tokens, vec, vec, mat, vec, mat, mat, vec, vec, vec, mat, vec, vec, vec,
        P(None, both), vec, vec, vec, mat, vec,
    )
    return jax.shard_map(body, mesh=mesh, in_specs=in_specs, out_specs=out_specs, check_vma=False)
```
